32 devices in a mesh: dp: 16 (over z, y, core), tensor: 2 (over x).
Axes of the slice: x: 2, y: 2, z: 4, core: 2. Of those that a mesh axis runs over, the one named last changes fastest.
Arguments:
- tokens: bfloat16 [16384, 768], P(('dp', 'tensor')), may hold values from -6 to 6
- encoded: bfloat16 [48, 512, 768], P('dp', 'tensor'), may hold values from -6 to 6
- cotangent: bfloat16 [16384, 768], P(('dp', 'tensor')), may hold values from -6 to 6
- segments: int32 [16, 1024], P('dp'), may hold values from 0 to 2, never falling along the last dimension, each value on 1 to 1022 neighbouring positions
- enc_lengths: int32 [48], P('dp'), may hold values from 128 to 512, as said below
- rel_buckets: int32 [1022], replicated, may hold values from 0 to 31, as said below
- gain_self: bfloat16 [768], P('dp'), may hold values from 0.5 to 1.5
- self_query: bfloat16 [768, 768], P('dp', 'tensor'), may hold values from -0.0546875 to 0.0546875
- self_key: bfloat16 [768, 768], P('dp', 'tensor'), may hold values from -0.21875 to 0.21875
- self_value: bfloat16 [768, 768], P('dp', 'tensor'), may hold values from -0.21875 to 0.21875
- self_out: bfloat16 [768, 768], P('dp', 'tensor'), may hold values from -1.25 to 1.25
- rel_table: float32 [32, 12], P(None, 'tensor'), may hold values from -4 to 4
- gain_cross: bfloat16 [768], P('dp'), may hold values from 0.5 to 1.5
- cross_query: bfloat16 [768, 768], P('dp', 'tensor'), may hold values from -0.0546875 to 0.0546875
- cross_key: bfloat16 [768, 768], P('dp', 'tensor'), may hold values from -0.21875 to 0.21875
- cross_value: bfloat16 [768, 768], P('dp', 'tensor'), may hold values from -0.21875 to 0.21875
- cross_out: bfloat16 [768, 768], P('dp', 'tensor'), may hold values from -1.25 to 1.25
- gain_ff: bfloat16 [768], P('dp'), may hold values from 0.5 to 1.5
- ff_gate: bfloat16 [768, 2048], P('dp', 'tensor'), may hold values from -0.21875 to 0.21875
- ff_up: bfloat16 [768, 2048], P('dp', 'tensor'), may hold values from -0.21875 to 0.21875
- ff_down: bfloat16 [768, 2048], P('dp', 'tensor'), may hold values from -0.125 to 0.125
Outputs:
- output: float32 [16384, 768], P(('dp', 'tensor'))
- grad_tokens: float32 [16384, 768], P(('dp', 'tensor'))
- grad_encoded: float32 [48, 512, 768], P('dp', 'tensor')
- grad_gain_self: float32 [768], P('dp')
- grad_self_query: float32 [768, 768], P('dp', 'tensor')
- grad_self_key: float32 [768, 768], P('dp', 'tensor')
- grad_self_value: float32 [768, 768], P('dp', 'tensor')
- grad_self_out: float32 [768, 768], P('dp', 'tensor')
- grad_rel_table: float32 [32, 12], P(None, 'tensor')
- grad_gain_cross: float32 [768], P('dp')
- grad_cross_query: float32 [768, 768], P('dp', 'tensor')
- grad_cross_key: float32 [768, 768], P('dp', 'tensor')
- grad_cross_value: float32 [768, 768], P('dp', 'tensor')
- grad_cross_out: float32 [768, 768], P('dp', 'tensor')
- grad_gain_ff: float32 [768], P('dp')
- grad_ff_gate: float32 [768, 2048], P('dp', 'tensor')
- grad_ff_up: float32 [768, 2048], P('dp', 'tensor')
- grad_ff_down: float32 [768, 2048], P('dp', 'tensor')
The draws below stay inside these ranges and needn't reach their ends.
Inputs may be any that keep to these rules, and one draw needn't show every extreme that they name: `segments`: sequence numbers never fall along a group, every number of 0 to 2 occurs, and no sequence has more than 1022 tokens; sequence s of group g reads encoder sequence g * 3 + s. `enc_lengths`: the live encoder tokens are the first ones of their sequence. rel_buckets[n] = n for n below 16; beyond that it never falls and rises by at most one from n to n + 1.
All inputs are finite; a program needn't handle non-finite values.
Results may differ from the reference program's by a relative error of at most 0.033.
Values may be sent and summed in bfloat16 or wider, within the bound.
No kernel may reach another device: no remote copies, remote signals or barrier semaphores. Data moves between devices by JAX's collectives and lax.ppermute only.
A program may use at most 384 MiB of HBM per device.

```python
import math
import jax
import jax.numpy as jnp
import numpy as np
from jax import lax

D = 768
H = 12
HD = 64
FF = 2048
BUCKETS = 32
ENC = 512
GROUP = 1024
SEGS = 3
MAXLEN = 1022
EXACT = 16
TOP = 31
HH = 768
TOKENS = 16384
ESEQ = 48
N_DP = 16


def draw_enc_lengths(key, part):
    lowest = max(1, ENC // 4)
    lengths = jax.random.randint(key, (ESEQ,), lowest, ENC + 1, dtype=jnp.int32)
    chosen = jax.random.randint(jax.random.fold_in(key, 7), (), 0, ESEQ, dtype=jnp.int32)
    return jnp.where(jnp.arange(ESEQ, dtype=jnp.int32) == chosen, ENC, lengths).astype(jnp.int32)


def draw_rel_buckets(key, part):
    rest_count = MAXLEN - EXACT
    rises = TOP - EXACT + 1
    order = jax.random.permutation(key, rest_count).astype(jnp.int32)
    marked = (order < rises).astype(jnp.int32)
    climbed = jnp.cumsum(marked).astype(jnp.int32)
    tail = (EXACT - 1 + climbed).astype(jnp.int32)
    head = jnp.arange(EXACT, dtype=jnp.int32)
    return jnp.concatenate((head, tail)).astype(jnp.int32)


def block_levels(own_key, extent, cuts, smallest, top_value):
    factor_of = 1.0
    for dim, shards_of in cuts:
        draws = jax.random.uniform(jax.random.fold_in(jax.random.fold_in(own_key, 6), dim), (shards_of,), jnp.float32, smallest / len(cuts), top_value / len(cuts))
        factor_of = factor_of * jnp.repeat(jnp.exp(draws), extent[dim] // shards_of).reshape((-1,) + (1,) * (len(extent) - 1 - dim))
    return factor_of


def length_profile(count, total, most, skew):
    portions = [(1 << 20) // math.isqrt(rank ** skew) + 1 for rank in range(2, count + 1)]
    spare, holding = total - most - (count - 1), [1] * (count - 1)
    while spare > 0:
        free = [i for i in range(count - 1) if holding[i] < most]
        mass, left = sum([portions[i] for i in free]), spare
        for i in free:
            extra = min(most - holding[i], max(1, left * portions[i] // mass), spare)
            holding[i] = holding[i] + extra
            spare = spare - extra
    return np.array([most] + holding)


def ragged_sizes(rng, count, total, reach, skew):
    if count == 2:
        one = jax.random.randint(rng, (), max(1, total - reach), min(reach, total - 1) + 1)
        return jnp.stack([one, total - one])
    tallies = jnp.asarray(length_profile(count, total, reach, skew), jnp.int32)
    couples = (count - 1) // 2
    source_of, taker = tallies[1:1 + 2 * couples:2], tallies[2:2 + 2 * couples:2]
    room = jnp.minimum(source_of - 1, reach - taker)
    shifted = jax.random.randint(jax.random.fold_in(rng, 1), (couples,), 0, 1 << 20) % (room + 1)
    tallies = tallies.at[1:1 + 2 * couples:2].set(source_of - shifted).at[2:2 + 2 * couples:2].set(taker + shifted)
    return tallies[jax.random.permutation(jax.random.fold_in(rng, 2), count)]


def bell_draw(own_key, shape, deviation, reach, shards=(), held_as=jnp.bfloat16):
    array = deviation * jax.random.normal(own_key, shape, jnp.float32)
    if shards:
        array = array * block_levels(own_key, shape, shards, -0.22, 0.18)
    return jnp.clip(array, -reach, reach).astype(held_as)


def setup_inputs(seed: int = 0) -> dict:
    seeds = jax.random.split(jax.random.key(seed), 22)
    return {
        "tokens": bell_draw(seeds[0], (TOKENS, D), 1.0, 6.0, ((0, 32),)),
        "encoded": bell_draw(seeds[1], (ESEQ, ENC, D), 1.0, 6.0, ((0, 16), (1, 2))),
        "cotangent": bell_draw(seeds[2], (TOKENS, D), 1.0, 6.0, ((0, 32),)),
        "segments": jax.vmap(lambda own: jnp.searchsorted(jnp.cumsum(ragged_sizes(own, SEGS, GROUP, MAXLEN, 2)), jnp.arange(GROUP), side="right"))(jax.random.split(seeds[3], N_DP)).reshape((N_DP, GROUP)).astype(jnp.int32),
        "enc_lengths": draw_enc_lengths(jax.random.fold_in(seeds[21], 71), 0),
        "rel_buckets": draw_rel_buckets(jax.random.fold_in(seeds[21], 71), 0),
        "gain_self": jnp.clip(1.0 + 0.1 * jax.random.normal(seeds[6], (D,), jnp.float32), 0.5, 1.5).astype(jnp.bfloat16),
        "self_query": bell_draw(seeds[7], (D, HH), (16 * D) ** -0.5, 0.0546875, ((0, 16), (1, 2))),
        "self_key": bell_draw(seeds[8], (D, HH), D ** -0.5, 0.21875, ((0, 16), (1, 2))),
        "self_value": bell_draw(seeds[9], (D, HH), D ** -0.5, 0.21875, ((0, 16), (1, 2))),
        "self_out": bell_draw(seeds[10], (D, HH), (HH // 32) ** -0.5, 1.25, ((0, 16), (1, 2))),
        "rel_table": bell_draw(seeds[11], (BUCKETS, H), 1.0, 4.0, ((1, 2),), jnp.float32),
        "gain_cross": jnp.clip(1.0 + 0.1 * jax.random.normal(seeds[12], (D,), jnp.float32), 0.5, 1.5).astype(jnp.bfloat16),
        "cross_query": bell_draw(seeds[13], (D, HH), (16 * D) ** -0.5, 0.0546875, ((0, 16), (1, 2))),
        "cross_key": bell_draw(seeds[14], (D, HH), D ** -0.5, 0.21875, ((0, 16), (1, 2))),
        "cross_value": bell_draw(seeds[15], (D, HH), D ** -0.5, 0.21875, ((0, 16), (1, 2))),
        "cross_out": bell_draw(seeds[16], (D, HH), (HH // 32) ** -0.5, 1.25, ((0, 16), (1, 2))),
        "gain_ff": jnp.clip(1.0 + 0.1 * jax.random.normal(seeds[17], (D,), jnp.float32), 0.5, 1.5).astype(jnp.bfloat16),
        "ff_gate": bell_draw(seeds[18], (D, FF), D ** -0.5, 0.21875, ((0, 16), (1, 2))),
        "ff_up": bell_draw(seeds[19], (D, FF), D ** -0.5, 0.21875, ((0, 16), (1, 2))),
        "ff_down": bell_draw(seeds[20], (D, FF), FF ** -0.5, 0.125, ((0, 16), (1, 2))),
    }


@jax.custom_vjp
def low(v):
    return lax.optimization_barrier(v.astype(jnp.bfloat16)).astype(jnp.float32)

@jax.custom_vjp
def low_back(v):
    return v

def low_keep(v):
    return (low(v), None)

def low_pass(kept, grad):
    return (grad,)

def back_keep(v):
    return (v, None)

def back_low(kept, grad):
    return (low(grad),)
low.defvjp(low_keep, low_pass)
low_back.defvjp(back_keep, back_low)
epsilon = 1e-06
masked_out = -1000000000.0
highest_precision = lax.Precision.HIGHEST

def multiply(left, right):
    return jnp.dot(left, right, precision=highest_precision, preferred_element_type=jnp.float32)

def rounded(vector):
    return low(low_back(vector))

def rms_norm(vector, gain_row):
    scaling = lax.rsqrt(lax.optimization_barrier(jnp.mean(vector * vector, axis=-1, keepdims=True)) + epsilon)
    return low(vector * scaling * gain_row)

def attend(queries, key_rows, value_rows, bias_of, allowed):
    query3 = queries.reshape(queries.shape[0], H, HD)
    key3 = key_rows.reshape(key_rows.shape[0], H, HD)
    value3 = value_rows.reshape(value_rows.shape[0], H, HD)
    scores = jnp.einsum('qhd,khd->hqk', query3, key3, precision=highest_precision) + bias_of
    scores = jnp.where(allowed[None], low_back(scores), masked_out)
    row_max = lax.optimization_barrier(jnp.max(scores, axis=-1, keepdims=True))
    exponent = jnp.exp(scores - row_max)
    softened = exponent / lax.optimization_barrier(jnp.sum(exponent, axis=-1, keepdims=True))
    mixture = jnp.einsum('hqk,khd->qhd', low(softened), value3, precision=highest_precision)
    return rounded(mixture.reshape(queries.shape[0], H * HD))

def layer(params, row_data, states, segment, enc_lens, rel_buckets):
    gain_self, self_query, self_key, self_value, self_out, rel_table, gain_cross, cross_query, cross_key, cross_value, cross_out, gain_ff, ff_gate, ff_up, ff_down = params
    position = jnp.arange(GROUP, dtype=jnp.int32)
    distance = position[:, None] - position[None, :]
    allowed = (distance >= 0) & (segment[:, None] == segment[None, :])
    bucket = rel_buckets[jnp.clip(distance, 0, MAXLEN - 1).astype(jnp.int32)]
    bias_of = jnp.transpose(rel_table)[:, bucket]
    normed_one = rms_norm(row_data, gain_self)
    attended = attend(rounded(multiply(normed_one, self_query)), rounded(multiply(normed_one, self_key)), rounded(multiply(normed_one, self_value)), bias_of, allowed)
    hidden_one = row_data + low_back(multiply(attended, jnp.transpose(self_out)))
    normed_two = rms_norm(hidden_one, gain_cross)
    key_place = jnp.arange(SEGS * ENC, dtype=jnp.int32)
    key_seq = key_place // ENC
    live = key_place % ENC < enc_lens[key_seq]
    allowed_cross = (segment[:, None] == key_seq[None, :]) & live[None, :]
    crossed = attend(rounded(multiply(normed_two, cross_query)), rounded(multiply(states, cross_key)), rounded(multiply(states, cross_value)), jnp.float32(0.0), allowed_cross)
    hidden_two = hidden_one + low_back(multiply(crossed, jnp.transpose(cross_out)))
    normed_three = rms_norm(hidden_two, gain_ff)
    gate_part = rounded(multiply(normed_three, ff_gate))
    up_part = rounded(multiply(normed_three, ff_up))
    hidden = low(jax.nn.gelu(gate_part, approximate=True) * up_part)
    return hidden_two + low_back(multiply(hidden, jnp.transpose(ff_down)))

def reference(tokens, encoded, cotangent, segments, enc_lengths, rel_buckets, gain_self, self_query, self_key, self_value, self_out, rel_table, gain_cross, cross_query, cross_key, cross_value, cross_out, gain_ff, ff_gate, ff_up, ff_down):
    params = tuple((item.astype(jnp.float32) for item in (gain_self, self_query, self_key, self_value, self_out, rel_table, gain_cross, cross_query, cross_key, cross_value, cross_out, gain_ff, ff_gate, ff_up, ff_down)))
    rows_all = tokens.astype(jnp.float32).reshape(N_DP, GROUP, D)
    states_all = encoded.astype(jnp.float32).reshape(N_DP, SEGS * ENC, D)
    cot_all = cotangent.astype(jnp.float32).reshape(N_DP, GROUP, D)
    lens_all = enc_lengths.reshape(N_DP, SEGS)

    def step(totals, item):
        row_data, states, cot_rows, segment, enc_lens = item

        def forward(weights, rows_in, states_in):
            return layer(weights, rows_in, states_in, segment, enc_lens, rel_buckets)
        result, pull = jax.vjp(forward, params, row_data, states)
        d_params, d_rows, d_states = pull(cot_rows)
        return (jax.tree.map(jnp.add, totals, d_params), (result, d_rows, d_states))
    zeros = jax.tree.map(jnp.zeros_like, params)
    grads, (results, d_rows, d_states) = lax.scan(step, zeros, (rows_all, states_all, cot_all, segments, lens_all))
    return (results.reshape(TOKENS, D), d_rows.reshape(TOKENS, D), d_states.reshape(ESEQ, ENC, D), grads[0], grads[1], grads[2], grads[3], grads[4], grads[5], grads[6], grads[7], grads[8], grads[9], grads[10], grads[11], grads[12], grads[13], grads[14])
```

```python
import functools

import jax
import jax.numpy as jnp
from jax import lax
from jax.experimental import pallas as pl
from jax.experimental.pallas import tpu as pltpu
from jax.sharding import PartitionSpec as P

epsilon = 1e-06
low_score = -1e30
f32 = jnp.float32
bf16 = jnp.bfloat16
exact = lax.Precision.HIGHEST
QB = 256
TB = 128


def nn(left, right):
    return jnp.dot(left, right, preferred_element_type=f32)


def nt(left, right, precision=None):
    return lax.dot_general(
        left, right, (((1,), (1,)), ((), ())), preferred_element_type=f32, precision=precision
    )


def tn(left, right, precision=None):
    return lax.dot_general(
        left, right, (((0,), (0,)), ((), ())), preferred_element_type=f32, precision=precision
    )


def normalize(vector, gain_row):
    scaling = lax.rsqrt(jnp.mean(vector * vector, axis=1, keepdims=True) + epsilon)
    normed = vector * scaling
    return (normed, scaling, (normed * gain_row).astype(bf16))


def norm_back(upstream, normed, scaling, gain_row):
    direct = upstream * gain_row
    inner = jnp.mean(direct * normed, axis=1, keepdims=True)
    return (scaling * (direct - normed * inner), jnp.sum(upstream * normed, axis=0, keepdims=True))


def flipped(value):
    return jnp.transpose(value.astype(f32)).astype(bf16)


def head_only(value, head, size):
    lane = lax.broadcasted_iota(jnp.int32, value.shape, 1)
    return jnp.where(lane // size == head, value, jnp.zeros_like(value))


def toeplitz(bias_row, width):
    return pltpu.roll(
        jnp.broadcast_to(bias_row, (TB, width)), 0, 1, stride=1, stride_axis=0
    )


def self_tiles(query_block, rows):
    first = query_block * QB // TB
    own = [(j * TB, (first - j + 1) * TB, 0) for j in range((query_block + 1) * QB // TB)]
    shift = rows // TB
    peer = [(rows + j * TB, (shift + first - j + 1) * TB, 1) for j in range(rows // TB)]
    return own, peer


def tile_mask(rows_ref, peer, key_row, lanes):
    place = lax.broadcasted_iota(jnp.int32, (TB, QB), 0) + key_row
    low = rows_ref[2 * peer : 2 * peer + 1, lanes]
    high = rows_ref[2 * peer + 1 : 2 * peer + 2, lanes]
    return (place >= low) & (place <= high)


def self_forward_kernel(
    size, rows_ref, bias_ref, q_ref, k_ref, v_ref, o_ref, lse_ref, vt, toe, score, prob, out_t
):
    rows = q_ref.shape[0]
    width = toe.shape[1]
    vt[...] = flipped(v_ref[...])
    for head in range(q_ref.shape[1] // size):
        toe[...] = toeplitz(bias_ref[0, head : head + 1, :], width)
        q_head = head_only(q_ref[...], head, size)
        cols = slice(head * size, (head + 1) * size)
        for block in range(rows // QB):
            lanes = slice(block * QB, (block + 1) * QB)
            q_block = q_head[lanes]
            top = jnp.full((1, QB), low_score, f32)
            groups = self_tiles(block, rows)
            for group in groups:
                for key_row, bias_at, peer in group:
                    raw = nt(k_ref[key_row : key_row + TB, :], q_block)
                    raw = raw + toe[:, bias_at : bias_at + QB]
                    keep = tile_mask(rows_ref, peer, key_row - peer * rows, lanes)
                    raw = jnp.where(keep, raw, low_score)
                    score[key_row : key_row + TB, :] = raw
                    top = jnp.maximum(top, jnp.max(raw, axis=0, keepdims=True))
            total = jnp.zeros((1, QB), f32)
            mixed = jnp.zeros((size, QB), f32)
            for group in groups:
                for key_row, bias_at, peer in group:
                    weight = jnp.exp(score[key_row : key_row + TB, :] - top)
                    total = total + jnp.sum(weight, axis=0, keepdims=True)
                    prob[key_row : key_row + TB, :] = weight.astype(bf16)
                span = slice(group[0][0], group[-1][0] + TB)
                mixed = mixed + nn(vt[cols, span], prob[span, :])
            out_t[cols, lanes] = mixed / total
            lse_ref[0, head : head + 1, lanes] = top + jnp.log(total)
    o_ref[...] = jnp.transpose(out_t[...]).astype(bf16)


def row_products(grad, out, head, size):
    lane = lax.broadcasted_iota(jnp.int32, (8, grad.shape[1]), 1)
    picker = jnp.where(lane // size == head, 1.0, 0.0).astype(f32)
    both = grad.astype(f32) * out.astype(f32)
    return nt(picker, both, exact)[0:1, :]


def self_backward_kernel(
    size, rows_ref, bias_ref, q_ref, k_ref, v_ref, o_ref, g_ref, lse_ref,
    dq_ref, dk_ref, dv_ref, diag_ref,
    kt, toe, prob, grad, diag, dq_t, dk_sum, dv_sum,
):
    rows = q_ref.shape[0]
    width = toe.shape[1]
    kt[...] = flipped(k_ref[...])
    dk_sum[...] = jnp.zeros_like(dk_sum)
    dv_sum[...] = jnp.zeros_like(dv_sum)
    flip = (
        lax.broadcasted_iota(jnp.int32, (TB, TB), 0) + lax.broadcasted_iota(jnp.int32, (TB, TB), 1)
        == TB - 1
    ).astype(f32)
    for head in range(q_ref.shape[1] // size):
        toe[...] = toeplitz(bias_ref[0, head : head + 1, :], width)
        diag[...] = jnp.zeros_like(diag)
        q_head = head_only(q_ref[...], head, size)
        g_head = head_only(g_ref[...], head, size)
        inner = row_products(g_ref[...], o_ref[...], head, size)
        cols = slice(head * size, (head + 1) * size)
        for block in range(rows // QB):
            lanes = slice(block * QB, (block + 1) * QB)
            q_block = q_head[lanes]
            g_block = g_head[lanes]
            lse = lse_ref[0, head : head + 1, lanes]
            inner_block = inner[:, lanes]
            d_query = jnp.zeros((size, QB), f32)
            for group in self_tiles(block, rows):
                for key_row, bias_at, peer in group:
                    key = slice(key_row, key_row + TB)
                    raw = nt(k_ref[key, :], q_block) + toe[:, bias_at : bias_at + QB]
                    keep = tile_mask(rows_ref, peer, key_row - peer * rows, lanes)
                    weight = jnp.where(keep, jnp.exp(raw - lse), 0.0)
                    pull = weight * (nt(v_ref[key, :], g_block) - inner_block)
                    prob[key, :] = weight.astype(bf16)
                    grad[key, :] = pull.astype(bf16)
                    diag[:, bias_at : bias_at + QB] += pull
                span = slice(group[0][0], group[-1][0] + TB)
                dv_sum[span, :] += nn(prob[span, :], g_block)
                dk_sum[span, :] += nn(grad[span, :], q_block)
                d_query = d_query + nn(kt[cols, span], grad[span, :])
            dq_t[cols, lanes] = d_query
        turned = pltpu.roll(
            jnp.dot(flip, diag[...], precision=exact, preferred_element_type=f32),
            0, 1, stride=1, stride_axis=0,
        )
        diag_ref[0, head : head + 1, :] = jnp.sum(turned, axis=0, keepdims=True)
    dq_ref[...] = jnp.transpose(dq_t[...]).astype(bf16)
    dk_ref[...] = dk_sum[...].astype(bf16)
    dv_ref[...] = dv_sum[...].astype(bf16)


def cross_forward_kernel(
    size, flags_ref, seg_ref, q_ref, k_ref, v_ref, o_ref, lse_ref, vt, prob, out_t
):
    rows = q_ref.shape[0]
    sequences = flags_ref.shape[0]
    half = k_ref.shape[0] // (2 * sequences)
    vt[...] = flipped(v_ref[...])
    out_t[...] = jnp.zeros_like(out_t)
    lse_ref[...] = jnp.zeros_like(lse_ref)
    place = lax.broadcasted_iota(jnp.int32, (half, QB), 0)
    for block in range(rows // QB):
        lanes = slice(block * QB, (block + 1) * QB)
        for seq in range(sequences):

            @pl.when(flags_ref[seq, 2 + block] > 0)
            def body(block=block, seq=seq, lanes=lanes):
                mine = seg_ref[0:1, lanes] == seq
                for head in range(q_ref.shape[1] // size):
                    cols = slice(head * size, (head + 1) * size)
                    q_block = head_only(q_ref[lanes, :], head, size)
                    scores = []
                    for part in range(2):
                        start = (part * sequences + seq) * half
                        raw = nt(k_ref[start : start + half, :], q_block)
                        scores.append(jnp.where(place < flags_ref[seq, part], raw, low_score))
                    top = jnp.maximum(
                        jnp.max(scores[0], axis=0, keepdims=True),
                        jnp.max(scores[1], axis=0, keepdims=True),
                    )
                    total = jnp.zeros((1, QB), f32)
                    mixed = jnp.zeros((size, QB), f32)
                    for part in range(2):
                        start = (part * sequences + seq) * half
                        weight = jnp.exp(scores[part] - top)
                        total = total + jnp.sum(weight, axis=0, keepdims=True)
                        mixed = mixed + nn(vt[cols, start : start + half], weight.astype(bf16))
                    out_t[cols, lanes] = jnp.where(mine, mixed / total, out_t[cols, lanes])
                    lse_ref[0, head : head + 1, lanes] = jnp.where(
                        mine, top + jnp.log(total), lse_ref[0, head : head + 1, lanes]
                    )

    o_ref[...] = jnp.transpose(out_t[...]).astype(bf16)


def cross_backward_kernel(
    size, flags_ref, seg_ref, q_ref, k_ref, v_ref, o_ref, g_ref, lse_ref,
    dq_ref, dk_ref, dv_ref, kt, dq_t, dk_sum, dv_sum,
):
    rows = q_ref.shape[0]
    sequences = flags_ref.shape[0]
    half = k_ref.shape[0] // (2 * sequences)
    kt[...] = flipped(k_ref[...])
    dq_t[...] = jnp.zeros_like(dq_t)
    dk_sum[...] = jnp.zeros_like(dk_sum)
    dv_sum[...] = jnp.zeros_like(dv_sum)
    place = lax.broadcasted_iota(jnp.int32, (half, QB), 0)
    for block in range(rows // QB):
        lanes = slice(block * QB, (block + 1) * QB)
        inners = [
            row_products(g_ref[lanes, :], o_ref[lanes, :], head, size)
            for head in range(q_ref.shape[1] // size)
        ]
        for seq in range(sequences):

            @pl.when(flags_ref[seq, 2 + block] > 0)
            def body(block=block, seq=seq, lanes=lanes, inners=inners):
                mine = seg_ref[0:1, lanes] == seq
                for head in range(q_ref.shape[1] // size):
                    cols = slice(head * size, (head + 1) * size)
                    q_block = head_only(q_ref[lanes, :], head, size)
                    g_block = head_only(g_ref[lanes, :], head, size)
                    lse = lse_ref[0, head : head + 1, lanes]
                    for part in range(2):
                        start = (part * sequences + seq) * half
                        key = slice(start, start + half)
                        raw = nt(k_ref[key, :], q_block)
                        keep = (place < flags_ref[seq, part]) & mine
                        weight = jnp.where(keep, jnp.exp(raw - lse), 0.0)
                        pull = weight * (nt(v_ref[key, :], g_block) - inners[head])
                        pull = pull.astype(bf16)
                        dv_sum[key, :] += nn(weight.astype(bf16), g_block)
                        dk_sum[key, :] += nn(pull, q_block)
                        dq_t[cols, lanes] += nn(kt[cols, key], pull)

    dq_ref[...] = jnp.transpose(dq_t[...]).astype(bf16)
    dk_ref[...] = dk_sum[...].astype(bf16)
    dv_ref[...] = dv_sum[...].astype(bf16)


def column_spec(rows):
    return pl.BlockSpec((rows, TB), lambda p: (0, p))


def whole_spec(array):
    return pl.BlockSpec(array.shape, lambda p: (0,) * array.ndim)


def pair_spec(array):
    return pl.BlockSpec((1,) + array.shape[1:], lambda p: (p, 0, 0))


def cost(queries, keys, columns, products):
    return pl.CostEstimate(
        flops=4 * products * queries * keys * columns,
        bytes_accessed=8 * (queries + keys) * columns,
        transcendentals=queries * keys * columns // 64,
    )


params = pltpu.CompilerParams(vmem_limit_bytes=48 * 1024 * 1024)


def self_forward(size, rows_in, bias, q, k, v):
    rows, keys, pairs = q.shape[0], k.shape[0], q.shape[1] // TB
    lse_shape = jax.ShapeDtypeStruct((pairs, 8, rows), f32)
    return pl.pallas_call(
        functools.partial(self_forward_kernel, size),
        name="self_forward",
        grid=(pairs,),
        in_specs=[whole_spec(rows_in), pair_spec(bias), column_spec(rows), column_spec(keys),
                  column_spec(keys)],
        out_specs=[column_spec(rows), pair_spec(lse_shape)],
        out_shape=[jax.ShapeDtypeStruct(q.shape, bf16), lse_shape],
        scratch_shapes=[
            pltpu.VMEM((TB, keys), bf16),
            pltpu.VMEM((TB, bias.shape[2]), f32),
            pltpu.VMEM((keys, QB), f32),
            pltpu.VMEM((keys, QB), bf16),
            pltpu.VMEM((TB, rows), f32),
        ],
        compiler_params=params,
        cost_estimate=cost(rows, keys, q.shape[1], 2),
    )(rows_in, bias, q, k, v)


def self_backward(size, rows_in, bias, q, k, v, o, g, lse):
    rows, keys, pairs = q.shape[0], k.shape[0], q.shape[1] // TB
    diag_shape = jax.ShapeDtypeStruct((pairs, 8, bias.shape[2]), f32)
    return pl.pallas_call(
        functools.partial(self_backward_kernel, size),
        name="self_backward",
        grid=(pairs,),
        in_specs=[whole_spec(rows_in), pair_spec(bias), column_spec(rows), column_spec(keys),
                  column_spec(keys), column_spec(rows), column_spec(rows), pair_spec(lse)],
        out_specs=[column_spec(rows), column_spec(keys), column_spec(keys), pair_spec(diag_shape)],
        out_shape=[jax.ShapeDtypeStruct(q.shape, bf16), jax.ShapeDtypeStruct(k.shape, bf16),
                   jax.ShapeDtypeStruct(v.shape, bf16), diag_shape],
        scratch_shapes=[
            pltpu.VMEM((TB, keys), bf16),
            pltpu.VMEM((TB, bias.shape[2]), f32),
            pltpu.VMEM((keys, QB), bf16),
            pltpu.VMEM((keys, QB), bf16),
            pltpu.VMEM((TB, bias.shape[2]), f32),
            pltpu.VMEM((TB, rows), f32),
            pltpu.VMEM((keys, TB), f32),
            pltpu.VMEM((keys, TB), f32),
        ],
        compiler_params=params,
        cost_estimate=cost(rows, keys, q.shape[1], 5),
    )(rows_in, bias, q, k, v, o, g, lse)


def cross_forward(size, flags, seg, q, k, v):
    rows, keys, pairs = q.shape[0], k.shape[0], q.shape[1] // TB
    lse_shape = jax.ShapeDtypeStruct((pairs, 8, rows), f32)
    return pl.pallas_call(
        functools.partial(cross_forward_kernel, size),
        name="cross_forward",
        grid=(pairs,),
        in_specs=[pl.BlockSpec(memory_space=pltpu.SMEM), whole_spec(seg), column_spec(rows),
                  column_spec(keys), column_spec(keys)],
        out_specs=[column_spec(rows), pair_spec(lse_shape)],
        out_shape=[jax.ShapeDtypeStruct(q.shape, bf16), lse_shape],
        scratch_shapes=[
            pltpu.VMEM((TB, keys), bf16),
            pltpu.VMEM((keys, QB), bf16),
            pltpu.VMEM((TB, rows), f32),
        ],
        compiler_params=params,
        cost_estimate=cost(rows, keys // 3, q.shape[1], 2),
    )(flags, seg, q, k, v)


def cross_backward(size, flags, seg, q, k, v, o, g, lse):
    rows, keys, pairs = q.shape[0], k.shape[0], q.shape[1] // TB
    return pl.pallas_call(
        functools.partial(cross_backward_kernel, size),
        name="cross_backward",
        grid=(pairs,),
        in_specs=[pl.BlockSpec(memory_space=pltpu.SMEM), whole_spec(seg), column_spec(rows),
                  column_spec(keys), column_spec(keys), column_spec(rows), column_spec(rows),
                  pair_spec(lse)],
        out_specs=[column_spec(rows), column_spec(keys), column_spec(keys)],
        out_shape=[jax.ShapeDtypeStruct(q.shape, bf16), jax.ShapeDtypeStruct(k.shape, bf16),
                   jax.ShapeDtypeStruct(v.shape, bf16)],
        scratch_shapes=[
            pltpu.VMEM((TB, keys), bf16),
            pltpu.VMEM((TB, rows), f32),
            pltpu.VMEM((keys, TB), f32),
            pltpu.VMEM((keys, TB), f32),
        ],
        compiler_params=params,
        cost_estimate=cost(rows, keys // 3, q.shape[1], 5),
    )(flags, seg, q, k, v, o, g, lse)


def swap(value, step):
    if step == "x":
        return lax.ppermute(value, "tensor", [(0, 1), (1, 0)])
    count = lax.axis_size("dp")
    return lax.ppermute(value, "dp", [(i, i ^ (1 << step)) for i in range(count)])


def join_blocks(mine, theirs, sizes, bit, rows):
    before = 1
    for size in sizes[:bit]:
        before *= size
    after = rows
    for size in sizes[bit + 1 :]:
        after *= size
    shape = (before, 1, after, mine.shape[-1])
    both = jnp.concatenate((mine.reshape(shape), theirs.reshape(shape)), axis=1)
    return both.reshape(-1, mine.shape[-1])


def gather_weights(shards, paired, order, bits, gate=None):
    rows = shards[0].shape[0]
    widths = [s.shape[1] for s in shards]
    held = [jnp.concatenate(shards, axis=1)] if len(shards) > 1 else list(shards)
    if gate is not None:
        held = list(lax.optimization_barrier((held[0], gate)))[:1]
    sizes = [1] * bits
    split = False
    witness = None
    for index, step in enumerate(order):
        if index == len(order) - 1:
            witness = held[0]
        got = [swap(h, step) for h in held]
        if step == "x":
            cuts = []
            start = 0
            for width in widths:
                cuts.append(slice(start, start + width))
                start += width
            held = [
                jnp.concatenate((held[0][:, c], got[0][:, c]), axis=1) if p else held[0][:, c]
                for c, p in zip(cuts, paired)
            ]
            split = True
        else:
            held = [join_blocks(h, g, sizes, step, rows) for h, g in zip(held, got)]
            sizes[step] = 2
    return held, witness


def add_low(one, two):
    return (one.astype(f32) + two.astype(f32)).astype(bf16)


def scatter_grads(pieces, order, bits, rows):
    summed = [add_low(keep, swap(send, 0)) for keep, send in pieces]
    widths = [s.shape[1] // 2 for s in summed]
    halves = [
        jnp.concatenate([s[:, :w] for s, w in zip(summed, widths)], axis=1),
        jnp.concatenate([s[:, w:] for s, w in zip(summed, widths)], axis=1),
    ]
    sizes = [1] + [2] * (bits - 1)
    for index, step in enumerate(order):
        last = index == len(order) - 1
        plus = (lambda a, b: a.astype(f32) + b.astype(f32)) if last else add_low
        if step == "x":
            halves = [plus(halves[0], swap(halves[1], "x"))]
        else:
            before = 1
            for size in sizes[:step]:
                before *= size
            width = halves[0].shape[-1]
            cut = [h.reshape(before, 2, -1, width) for h in halves]
            got = [swap(c[:, 1].reshape(-1, width), step) for c in cut]
            halves = [plus(c[:, 0].reshape(-1, width), g) for c, g in zip(cut, got)]
            sizes[step] = 1
    total = halves[0]
    outs = []
    start = 0
    for width in widths:
        outs.append(total[:, start : start + width])
        start += width
    return outs


def split_tn(left, right):
    half = left.shape[1] // 2
    return (tn(left[:, :half], right).astype(bf16), tn(left[:, half:], right).astype(bf16))


def local(
    tokens,
    encoded,
    cotangent,
    segments,
    enc_lengths,
    rel_buckets,
    gain_self,
    self_query,
    self_key,
    self_value,
    self_out,
    rel_table,
    gain_cross,
    cross_query,
    cross_key,
    cross_value,
    cross_out,
    gain_ff,
    ff_gate,
    ff_up,
    ff_down,
):
    count = lax.axis_size("dp")
    bits = count.bit_length() - 1
    piece, head_cols = self_query.shape
    width = tokens.shape[1]
    rows = tokens.shape[0]
    head_local = rel_table.shape[1]
    heads = 2 * head_local
    size = head_cols // head_local
    pairs = heads * size // TB
    bucket_count = rel_table.shape[0]
    span = rel_buckets.shape[0]
    sequences, enc_half = encoded.shape[:2]
    dp_at = lax.axis_index("dp")
    tensor_at = lax.axis_index("tensor")
    far = list(range(2, bits))
    near_first = [["x", 1] + far, [1] + far + ["x"], far + ["x", 1]]
    gather_order = [list(reversed(o)) + [0] for o in near_first]

    feature = jnp.arange(width, dtype=jnp.int32)
    block = feature // piece
    mask = jnp.zeros_like(block)
    for bit in range(bits):
        mask = mask + (((block >> (bits - 1 - bit)) & 1) << bit)
    source = (dp_at.astype(jnp.int32) ^ mask) * piece + feature % piece
    shuffle = (feature[:, None] == source[None, :]).astype(bf16)

    def restore(values):
        high = values.astype(bf16)
        low = (values - high.astype(f32)).astype(bf16)
        return nt(high, shuffle) + nt(low, shuffle)

    gain_cols = jnp.pad(
        jnp.stack((gain_self, gain_cross, gain_ff), axis=1), ((0, 0), (0, TB - 3))
    )
    (w_query, gains), _ = gather_weights(
        [self_query, gain_cols], [True, False], gather_order[0], bits
    )
    (w_key,), wit_a = gather_weights([self_key], [True], gather_order[1], bits)
    (w_value,), wit_b = gather_weights([self_value], [True], gather_order[2], bits)
    (w_out,), _ = gather_weights([self_out], [True], gather_order[0], bits)
    (c_key, c_value), wit_c = gather_weights(
        [cross_key, cross_value], [True, True], gather_order[1], bits, wit_a
    )
    (c_query, c_out), wit_d = gather_weights(
        [cross_query, cross_out], [True, True], gather_order[2], bits, wit_b
    )
    (w_gate,), _ = gather_weights([ff_gate], [True], gather_order[0], bits, wit_b)
    (w_up,), _ = gather_weights([ff_up], [True], gather_order[1], bits, wit_c)
    (w_down,), _ = gather_weights([ff_down], [True], gather_order[2], bits, wit_d)
    pick = (
        lax.broadcasted_iota(jnp.int32, (8, TB), 0) == lax.broadcasted_iota(jnp.int32, (8, TB), 1)
    ).astype(bf16)
    gain_rows = nt(pick, gains)
    gain_s, gain_c, gain_f = gain_rows[0:1], gain_rows[1:2], gain_rows[2:3]

    token_all = nn(jnp.concatenate((tokens, swap(tokens, "x"))), shuffle).astype(bf16)
    enc_own = encoded.reshape(-1, width)
    states = nn(jnp.concatenate((enc_own, swap(enc_own, "x"))), shuffle).astype(bf16)
    d_branch = nn(cotangent, shuffle).astype(bf16)

    segment = segments[0]
    group_rows = segment.shape[0]
    position = jnp.arange(group_rows, dtype=jnp.int32)
    begins = jnp.sum((segment[None, :] < segment[:, None]).astype(jnp.int32), axis=1)
    base = tensor_at.astype(jnp.int32) * rows
    own_begin = lax.dynamic_slice_in_dim(begins, base, rows)
    own_segment = lax.dynamic_slice_in_dim(segment, base, rows)
    place = jnp.arange(rows, dtype=jnp.int32)
    peer_high = jnp.where(tensor_at == 1, rows - 1, -1).astype(jnp.int32)
    zero_row = jnp.zeros_like(place)
    rows_in = jnp.stack(
        (own_begin - base, place, own_begin - (rows - base), zero_row + peer_high)
        + (zero_row,) * 4
    )
    seg_in = jnp.broadcast_to(own_segment[None, :], (8, rows))
    wide = group_rows + TB
    bucket_of = jnp.pad(rel_buckets, (0, group_rows - span), mode="edge")
    chosen = (bucket_of[:, None] == jnp.arange(bucket_count)[None, :]).astype(f32)
    table = jnp.concatenate((rel_table, swap(rel_table, "x")), axis=1)
    bias = lax.dot_general(
        table, chosen, (((0,), (1,)), ((), ())), precision=exact, preferred_element_type=f32
    )
    bias = jnp.pad(bias, ((0, 0), (TB, 0))).reshape(pairs, -1, wide)
    seq_ids = jnp.arange(sequences, dtype=jnp.int32)
    blocks_of = own_segment.reshape(-1, QB)
    active = jnp.any(blocks_of[None] == seq_ids[:, None, None], axis=2).astype(jnp.int32)
    enc_base = tensor_at.astype(jnp.int32) * enc_half
    flags = jnp.concatenate(
        (
            (enc_lengths - enc_base)[:, None],
            (enc_lengths - (enc_half - enc_base))[:, None],
            active,
        ),
        axis=1,
    ).astype(jnp.int32)

    inputs_all = token_all.astype(f32)
    normed_all, scale_all, rows_one = normalize(inputs_all, gain_s)
    inputs, normed_one, scale_one = inputs_all[:rows], normed_all[:rows], scale_all[:rows]
    own_one = rows_one[:rows]
    query_s = nn(own_one, w_query).astype(bf16)
    key_s = nn(rows_one, w_key).astype(bf16)
    value_s = nn(rows_one, w_value).astype(bf16)
    attended, lse_s = self_forward(size, rows_in, bias, query_s, key_s, value_s)
    hidden_one = inputs + nt(attended, w_out)
    normed_two, scale_two, rows_two = normalize(hidden_one, gain_c)
    key_c = nn(states, c_key).astype(bf16)
    value_c = nn(states, c_value).astype(bf16)
    query_c = nn(rows_two, c_query).astype(bf16)
    crossed, lse_c = cross_forward(size, flags, seg_in, query_c, key_c, value_c)
    hidden_two = hidden_one + nt(crossed, c_out)
    normed_three, scale_three, rows_three = normalize(hidden_two, gain_f)
    gate_part = nn(rows_three, w_gate).astype(bf16)
    up_part = nn(rows_three, w_up).astype(bf16)
    activated, gelu_pull = jax.vjp(
        lambda gate_in: jax.nn.gelu(gate_in, approximate=True), gate_part.astype(f32)
    )
    up_float = up_part.astype(f32)
    hidden = (activated * up_float).astype(bf16)
    output = restore(hidden_two + nt(hidden, w_down))

    d_hidden = nn(d_branch, w_down)
    (d_gate,) = gelu_pull(d_hidden * up_float)
    d_gate = d_gate.astype(bf16)
    d_up = (d_hidden * activated).astype(bf16)
    (g_down,) = scatter_grads([split_tn(d_branch, hidden)], near_first[2], bits, piece)
    (g_gate,) = scatter_grads([split_tn(rows_three, d_gate)], near_first[0], bits, piece)
    (g_up,) = scatter_grads([split_tn(rows_three, d_up)], near_first[1], bits, piece)
    d_normed_three = nt(d_gate, w_gate) + nt(d_up, w_up)
    d_through, d_gain_f = norm_back(d_normed_three, normed_three, scale_three, gain_f)
    d_hidden_two = d_branch.astype(f32) + d_through

    d_branch_two = d_hidden_two.astype(bf16)
    d_crossed = nn(d_branch_two, c_out).astype(bf16)
    d_query_c, d_key_c, d_value_c = cross_backward(
        size, flags, seg_in, query_c, key_c, value_c, crossed, d_crossed, lse_c
    )
    g_c_out, g_c_query = scatter_grads(
        [split_tn(d_branch_two, crossed), split_tn(rows_two, d_query_c)], near_first[0], bits, piece
    )
    g_c_key, g_c_value = scatter_grads(
        [split_tn(states, d_key_c), split_tn(states, d_value_c)], near_first[1], bits, piece
    )
    d_normed_two = nt(d_query_c, c_query)
    d_through_two, d_gain_c = norm_back(d_normed_two, normed_two, scale_two, gain_c)
    d_hidden_one = d_hidden_two + d_through_two
    d_states = nt(d_key_c, c_key) + nt(d_value_c, c_value)
    enc_rows = enc_own.shape[0]
    d_states_own = d_states[:enc_rows] + swap(d_states[enc_rows:].astype(bf16), "x").astype(f32)
    grad_encoded = restore(d_states_own).reshape(encoded.shape)

    d_branch_one = d_hidden_one.astype(bf16)
    d_attended = nn(d_branch_one, w_out).astype(bf16)
    d_query_s, d_key_s, d_value_s, diagonals = self_backward(
        size, rows_in, bias, query_s, key_s, value_s, attended, d_attended, lse_s
    )
    (g_s_out,) = scatter_grads([split_tn(d_branch_one, attended)], near_first[2], bits, piece)
    d_normed_one = (
        nt(d_key_s[rows:], w_key) + nt(d_value_s[rows:], w_value)
    ).astype(bf16)
    d_normed_own = (
        nt(d_query_s, w_query) + nt(d_key_s[:rows], w_key) + nt(d_value_s[:rows], w_value)
    ) + swap(d_normed_one, "x").astype(f32)
    d_through_one, d_gain_s = norm_back(d_normed_own, normed_one, scale_one, gain_s)
    grad_tokens = restore(d_hidden_one + d_through_one)

    by_distance = jnp.roll(diagonals[:, : heads // pairs].reshape(heads, wide), 1 - 2 * TB, axis=1)
    d_table = lax.dot_general(
        chosen, by_distance[:, :group_rows], (((0,), (1,)), ((), ())),
        precision=exact, preferred_element_type=f32,
    )
    d_gains = jnp.concatenate((d_gain_s, d_gain_c, d_gain_f) + (jnp.zeros_like(d_gain_s),) * 5)
    gain_back = tn(d_gains, pick.astype(f32), exact)
    cells = bucket_count * head_local
    per_row = -(-cells // piece)

    def small_columns(part):
        flat = jnp.pad(part.reshape(-1), (0, per_row * piece - cells)).reshape(piece, per_row)
        tiled = jnp.tile(flat, (count, 1))
        return gain_back + jnp.pad(tiled, ((0, 0), (8, TB - 8 - per_row)))

    small = jnp.concatenate(
        (small_columns(d_table[:, :head_local]), small_columns(d_table[:, head_local:])), axis=1
    ).astype(bf16)
    half = width // 2
    g_s_query, g_small = scatter_grads(
        [split_tn(own_one, d_query_s), (small[:half], small[half:])], near_first[0], bits, piece
    )
    (g_s_key,) = scatter_grads([split_tn(rows_one, d_key_s)], near_first[1], bits, piece)
    (g_s_value,) = scatter_grads([split_tn(rows_one, d_value_s)], near_first[2], bits, piece)
    grad_table = g_small[:, 8 : 8 + per_row].reshape(-1)[:cells].reshape(bucket_count, head_local)
    return (
        output,
        grad_tokens,
        grad_encoded,
        g_small[:, 0],
        g_s_query,
        g_s_key,
        g_s_value,
        g_s_out,
        grad_table,
        g_small[:, 1],
        g_c_query,
        g_c_key,
        g_c_value,
        g_c_out,
        g_small[:, 2],
        g_gate,
        g_up,
        g_down,
    )


def solution(mesh):
    in_specs = (
        P(("dp", "tensor"), None),
        P("dp", "tensor", None),
        P(("dp", "tensor"), None),
        P("dp", None),
        P("dp"),
        P(),
        P("dp"),
        P("dp", "tensor"),
        P("dp", "tensor"),
        P("dp", "tensor"),
        P("dp", "tensor"),
        P(None, "tensor"),
        P("dp"),
        P("dp", "tensor"),
        P("dp", "tensor"),
        P("dp", "tensor"),
        P("dp", "tensor"),
        P("dp"),
        P("dp", "tensor"),
        P("dp", "tensor"),
        P("dp", "tensor"),
    )
    out_specs = (
        P(("dp", "tensor"), None),
        P(("dp", "tensor"), None),
        P("dp", "tensor", None),
        P("dp"),
        P("dp", "tensor"),
        P("dp", "tensor"),
        P("dp", "tensor"),
        P("dp", "tensor"),
        P(None, "tensor"),
        P("dp"),
        P("dp", "tensor"),
        P("dp", "tensor"),
        P("dp", "tensor"),
        P("dp", "tensor"),
        P("dp"),
        P("dp", "tensor"),
        P("dp", "tensor"),
        P("dp", "tensor"),
    )
    return jax.shard_map(local, mesh=mesh, in_specs=in_specs, out_specs=out_specs, check_vma=False)
```
